32 devices in a mesh: groups: 2 (over y), seq: 16 (over z, x, core).
Axes of the slice: x: 2, y: 2, z: 4, core: 2. Of those that a mesh axis runs over, the one named last changes fastest.
Arguments:
- key_values: bfloat16 [3, 2048, 8192], P(None, 'seq', 'groups'), parts along dimension 2, may hold values from -14 to 14, as said below
- bases: bfloat16 [3, 2, 1024, 256], replicated, may hold values from -0.1875 to 0.1875
- owner_slots: int32 [3, 64], P(None, ('groups', 'seq')), parts along dimension 1, may hold values from 0 to 15, as said below
Outputs:
- received: bfloat16 [512, 512, 128], P(('groups', 'seq')), parts along dimension 0
- grams: float32 [6, 2, 256, 256], P('groups'), parts along dimension 0
- energies: float32 [6, 2, 1024], P('groups'), parts along dimension 0
The draws below stay inside these ranges and needn't reach their ends.
There are 2 independent parts, one for each index of `groups`. The reference program is written for one: setup_inputs(seed, part) draws one part's arguments, and reference() takes and returns one part's arrays. A program takes and returns all parts, laid end to end along the dimension named above; an argument that names none is the same for every part. Nothing has to cross between parts.
Inputs may be any that keep to these rules, and one draw needn't show every extreme that they name: key_values are finite real values within the range. `owner_slots`: block j of a layer belongs to device j // 2 of seq; the 6 values of one device's blocks over all layers are distinct, so an owner's slot is written at most once; some owner has all 16 slots filled.
All inputs are finite; a program needn't handle non-finite values.
Results may differ from the reference program's by a relative error of at most 0.001.
Values may be sent and summed in bfloat16 or wider, within the bound.
A program may use at most 128 MiB of HBM per device.

```python
import jax
import jax.numpy as jnp

KW = 1024
RANK = 256
L = 3
BLOCK = 128
REACH = 8
TOK_DEV = 256
BLK_DEV = 2
OWNER_SLOT_LIMIT = 2
CAP = 16
TOKENS = 4096
NBLK = 32
N_SEQ = 16


def draw_key_values(key, part):
    key_main = jax.random.fold_in(key, 3)
    ramp = 0.6 + 1.2 * jnp.arange(TOKENS, dtype=jnp.float32) / TOKENS
    values = jax.random.truncated_normal(key_main, -4.0, 4.0, (L, 2 * KW, TOKENS), jnp.float32)
    values = values * ramp[None, None, :]
    return values.astype(jnp.bfloat16)


def draw_owner_slots(key, part):
    key_perm = jax.random.fold_in(key, 11)
    key_root = jax.random.fold_in(key, 12)
    key_order = jax.random.fold_in(key, 13)
    slot_total_count = CAP
    unit_count = L * (TOK_DEV // BLOCK)
    root_owner = jax.random.randint(key_root, (), 0, N_SEQ)
    device_ids = jnp.arange(N_SEQ, dtype=jnp.int32)
    destination_offset = (root_owner - device_ids) % N_SEQ
    mandatory_pick = destination_offset < REACH
    ranking_numbers = jax.vmap(lambda subkey: jax.random.permutation(subkey, slot_total_count))(jax.random.split(key_perm, N_SEQ))
    slot_index_list = jnp.arange(slot_total_count, dtype=jnp.int32)
    extra_priority = jnp.where(mandatory_pick[:, None] & (slot_index_list[None, :] // OWNER_SLOT_LIMIT == destination_offset[:, None]), slot_total_count, 0)
    priority_list = ranking_numbers + extra_priority
    ordering = jnp.argsort(-priority_list, axis=1, stable=True)
    chosen = ordering[:, :unit_count]
    shuffle = jax.vmap(lambda subkey: jax.random.permutation(subkey, unit_count))(jax.random.split(key_order, N_SEQ))
    chosen = jnp.take_along_axis(chosen, shuffle, axis=1)
    chosen = chosen.reshape(N_SEQ, L, TOK_DEV // BLOCK).transpose(1, 0, 2)
    return chosen.reshape(L, N_SEQ * (TOK_DEV // BLOCK)).astype(jnp.int32)


def normal_values(key, shape, width, limit, held_as=jnp.bfloat16):
    values = width * jax.random.normal(key, shape, jnp.float32)
    return jnp.clip(values, min=-limit, max=limit).astype(held_as)


def setup_inputs(seed: int = 0, part: int = 0) -> dict:
    keys = jax.random.split(jax.random.key(seed), 4)
    own_keys = jax.random.split(jax.random.fold_in(keys[3], part), 4)
    key_values = draw_key_values(jax.random.fold_in(jax.random.fold_in(keys[3], part), 71), part)
    bases = normal_values(keys[1], (L, 2, KW, RANK), KW ** -0.5, 0.1875)
    owner_slots = draw_owner_slots(jax.random.fold_in(jax.random.fold_in(keys[3], part), 71), part)
    return dict(key_values=key_values, bases=bases, owner_slots=owner_slots)


def reference(key_values, bases, owner_slots):
    tokens = key_values.shape[2]
    gram_list = []
    energy_list = []
    block_list = []
    for layer_idx in range(L):
        layer_grams = []
        layer_energy = []
        layer_coeff = []
        for side in range(2):
            slab_rows = key_values[layer_idx, side * KW:(side + 1) * KW, :]
            basis = bases[layer_idx, side]
            coeff = jnp.dot(basis.T, slab_rows, preferred_element_type=jnp.float32).astype(jnp.bfloat16)
            recon = jnp.dot(basis, coeff, preferred_element_type=jnp.float32)
            resid = slab_rows.astype(jnp.float32) - recon
            layer_energy.append(jnp.sum(resid * resid, axis=1) / tokens)
            layer_grams.append(jnp.dot(coeff, coeff.T, preferred_element_type=jnp.float32) / tokens)
            layer_coeff.append(coeff)
        gram_list.append(jnp.stack(layer_grams))
        energy_list.append(jnp.stack(layer_energy))
        joined = jnp.concatenate(layer_coeff, axis=0)
        block_list.append(joined.reshape(2 * RANK, NBLK, BLOCK).transpose(1, 0, 2))
    units = jnp.stack(block_list).reshape(L * NBLK, 2 * RANK, BLOCK)
    block_ids = jnp.arange(NBLK, dtype=jnp.int32)[None, :]
    device_ids = block_ids // BLK_DEV
    owners = (device_ids + owner_slots // OWNER_SLOT_LIMIT) % N_SEQ
    targets = (owners * CAP + owner_slots).astype(jnp.int32).reshape(-1)
    received = jnp.zeros((N_SEQ * CAP, 2 * RANK, BLOCK), jnp.bfloat16).at[targets].set(units)
    return received, jnp.stack(gram_list), jnp.stack(energy_list)
```

```python
import functools

import jax
import jax.numpy as jnp
from jax import lax
from jax.experimental import pallas as pl
from jax.experimental.pallas import tpu as pltpu
from jax.sharding import PartitionSpec as P

REACH = 8
OWNER_SLOT_LIMIT = 2
CAP = 16
LANES = 128
MESH = pl.DeviceIdType.MESH


def loop(lo, hi, body):
    def step(i, carry):
        body(i)
        return carry

    lax.fori_loop(lo, hi, step, 0)


def kernel(
    n, layers, width, rank, span, piece, tokens,
    kv_ref, bases_ref, slot_ref,
    recv_ref, grams_ref, energies_ref,
    x_buf, basis_buf, coeff_buf, out_buf, slot_mine, slot_buf, part_buf, sum_buf, full_buf,
    basis_sem, own_sem, x_send, x_recv, slot_send, slot_recv, slot_own,
    rs_send, rs_recv, ag_send, ag_recv, mir_send, mir_recv, fwd_send, fwd_recv,
    out_send, out_recv, out_own,
):
    m = n // 2
    chunk = 2 * width // n
    me = lax.axis_index("seq")
    side = me // m
    q = lax.rem(me, m)
    base = side * m
    lrows = 2 * rank + width // LANES

    def remote(src, dst, send, recv, dev):
        return pltpu.make_async_remote_copy(
            src_ref=src, dst_ref=dst, send_sem=send, recv_sem=recv,
            device_id={"seq": dev}, device_id_type=MESH,
        )

    def basis_copy(l):
        return pltpu.make_async_copy(bases_ref.at[l, side], basis_buf.at[l], basis_sem.at[l])

    def own_copy(l):
        return pltpu.make_async_copy(
            kv_ref.at[l, :, pl.ds(pl.multiple_of(q * span, span), span)],
            x_buf.at[l, pl.ds(pl.multiple_of(q * chunk, chunk), chunk), :],
            own_sem.at[l],
        )

    def x_copy(l, r):
        to = lax.rem(q + r, m)
        return remote(
            kv_ref.at[l, :, pl.ds(pl.multiple_of(to * span, span), span)],
            x_buf.at[l, pl.ds(pl.multiple_of(q * chunk, chunk), chunk), :],
            x_send.at[l, r], x_recv.at[l, r], base + to,
        )

    barrier = pltpu.get_barrier_semaphore()

    def greet(r):
        pl.semaphore_signal(
            barrier, inc=1, device_id={"seq": lax.rem(me + r, n)}, device_id_type=MESH
        )

    for l in range(layers):
        basis_copy(l).start()
        own_copy(l).start()
    slot_mine[...] = jnp.zeros(slot_mine.shape, jnp.int32)
    for l in range(layers):
        for b in range(2):
            slot_mine[2 * l + b : 2 * l + b + 1, :] = jnp.full((1, LANES), slot_ref[l, b], jnp.int32)
    loop(1, n, greet)
    pl.semaphore_wait(barrier, n - 1)

    for l in range(layers):
        loop(1, m, lambda r: x_copy(l, r).start())

    lower = lax.rem(me, 2)

    def slot_copy(hh):
        return remote(
            slot_mine, slot_buf.at[lower], slot_send.at[hh], slot_recv.at[lower], hh * m + me // 2
        )

    def slot_local():
        return pltpu.make_async_copy(slot_mine, slot_buf.at[lower], slot_own)

    for hh in range(2):

        @pl.when(hh * m + me // 2 != me)
        def _():
            slot_copy(hh).start()

        @pl.when(hh * m + me // 2 == me)
        def _():
            slot_local().start()

    for l in range(layers):
        basis_copy(l).wait()
        own_copy(l).wait()
        loop(1, m, lambda r: x_copy(l, r).wait_recv())
        coeff = lax.dot_general(
            basis_buf[l], x_buf[l], (((0,), (0,)), ((), ())), preferred_element_type=jnp.float32
        ).astype(jnp.bfloat16)
        coeff_buf[l] = coeff
        gram = lax.dot_general(
            coeff, coeff, (((1,), (1,)), ((), ())), preferred_element_type=jnp.float32
        )
        top = l * lrows
        for j in range(rank // LANES):
            part_buf[top + j * rank : top + (j + 1) * rank, :] = gram[:, j * LANES : (j + 1) * LANES]
        top += 2 * rank
        rows = 256
        for c in range(width // rows):
            recon = jnp.dot(
                basis_buf[l, c * rows : (c + 1) * rows, :], coeff, preferred_element_type=jnp.float32
            )
            resid = x_buf[l, c * rows : (c + 1) * rows, :].astype(jnp.float32) - recon
            square = resid * resid
            folded = square[:, :LANES]
            for j in range(1, span // LANES):
                folded = folded + square[:, j * LANES : (j + 1) * LANES]
            line = jnp.sum(folded.T, axis=0, keepdims=True)
            for j in range(rows // LANES):
                at = top + c * (rows // LANES) + j
                part_buf[at : at + 1, :] = line[:, j * LANES : (j + 1) * LANES]

    total_rows = m * piece
    if total_rows > layers * lrows:
        part_buf[layers * lrows :, :] = jnp.zeros(
            (total_rows - layers * lrows, LANES), jnp.float32
        )

    def rows_of(i):
        return pl.ds(pl.multiple_of(i * piece, piece), piece)

    def rs_copy(r):
        to = lax.rem(q + r, m)
        return remote(
            part_buf.at[rows_of(to), :], sum_buf.at[r], rs_send.at[r], rs_recv.at[r], base + to
        )

    loop(1, m, lambda r: rs_copy(r).start())

    def slot_from(dd):
        return lax.rem(2 * q + dd, n)

    for dd in range(2):
        src_dev = 2 * q + dd

        @pl.when(src_dev != me)
        def _():
            remote(slot_mine, slot_buf.at[dd], slot_send.at[0], slot_recv.at[dd], me).wait_recv()

        @pl.when(src_dev == me)
        def _():
            pltpu.make_async_copy(slot_mine, slot_buf.at[dd], slot_own).wait()

    def out_dst(k):
        return recv_ref.at[
            pl.ds(OWNER_SLOT_LIMIT * k, OWNER_SLOT_LIMIT),
            pl.ds(pl.multiple_of(side * rank, rank), rank),
            :,
        ]

    def out_copy(dd, k):
        to = lax.rem(2 * q + dd + k, n)
        return remote(
            out_buf.at[dd, pl.ds(OWNER_SLOT_LIMIT * k, OWNER_SLOT_LIMIT)], out_dst(k),
            out_send.at[dd, k], out_recv.at[side, k], to,
        )

    def out_local(dd, k):
        return pltpu.make_async_copy(
            out_buf.at[dd, pl.ds(OWNER_SLOT_LIMIT * k, OWNER_SLOT_LIMIT)], out_dst(k), out_own.at[dd]
        )

    for k in reversed(range(REACH)):
        for dd in range(2):
            for w in range(OWNER_SLOT_LIMIT):
                v = OWNER_SLOT_LIMIT * k + w
                acc = None
                for l in range(layers):
                    for b in range(2):
                        pick = slot_buf[dd, 2 * l + b : 2 * l + b + 1, :] == v
                        pick = pick.astype(jnp.float32).astype(jnp.bfloat16)
                        at = (2 * dd + b) * LANES
                        term = coeff_buf[l, :, at : at + LANES] * pick
                        acc = term if acc is None else acc + term
                out_buf[dd, v] = acc
            to = lax.rem(2 * q + dd + k, n)

            @pl.when(to != me)
            def _():
                out_copy(dd, k).start()

            @pl.when(to == me)
            def _():
                out_local(dd, k).start()

    loop(1, m, lambda r: rs_copy(r).wait())
    total = part_buf[rows_of(q), :]
    for r in range(1, m):
        total = total + sum_buf[r]
    full_buf[side, rows_of(q), :] = total

    def ag_copy(r):
        at = full_buf.at[side, rows_of(q), :]
        return remote(at, at, ag_send.at[r], ag_recv.at[r], base + lax.rem(q + r, m))

    def mirror_copy():
        at = full_buf.at[side, rows_of(q), :]
        return remote(at, at, mir_send, mir_recv, (1 - side) * m + q)

    def fwd_copy(r):
        at = full_buf.at[1 - side, rows_of(q), :]
        return remote(at, at, fwd_send.at[r], fwd_recv.at[r], base + lax.rem(q + r, m))

    mirror_copy().start()
    loop(1, m, lambda r: ag_copy(r).start())
    mirror_copy().wait()
    loop(1, m, lambda r: fwd_copy(r).start())
    loop(1, m, lambda r: ag_copy(r).wait())
    loop(1, m, lambda r: fwd_copy(r).wait())

    scale = 1.0 / tokens
    for s in range(2):
        for l in range(layers):
            top = l * lrows
            for j in range(rank // LANES):
                grams_ref[l, s, :, j * LANES : (j + 1) * LANES] = (
                    full_buf[s, top + j * rank : top + (j + 1) * rank, :] * scale
                )
            top += 2 * rank
            for j in range(width // LANES):
                energies_ref[l, s : s + 1, j * LANES : (j + 1) * LANES] = (
                    full_buf[s, top + j : top + j + 1, :] * scale
                )

    for hh in range(2):

        @pl.when(hh * m + me // 2 != me)
        def _():
            slot_copy(hh).wait_send()

    for l in range(layers):
        loop(1, m, lambda r: x_copy(l, r).wait_send())
    for dd in range(2):
        for k in range(REACH):
            to = lax.rem(2 * q + dd + k, n)

            @pl.when(to != me)
            def _():
                out_copy(dd, k).wait_send()

            @pl.when(to == me)
            def _():
                out_local(dd, k).wait()

    for hh in range(2):
        for k in range(REACH):
            sender = hh * m + lax.rem(me - k + n, n) // 2

            @pl.when(sender != me)
            def _():
                at = recv_ref.at[
                    pl.ds(OWNER_SLOT_LIMIT * k, OWNER_SLOT_LIMIT), pl.ds(hh * rank, rank), :
                ]
                remote(at, at, out_send.at[0, 0], out_recv.at[hh, k], me).wait_recv()


def per_device(key_values, bases, owner_slots):
    n = lax.axis_size("seq")
    layers, chunk, tokens = key_values.shape
    width, rank = bases.shape[2], bases.shape[3]
    m = n // 2
    span = tokens // m
    lrows = 2 * rank + width // LANES
    piece = -(-layers * lrows // (8 * m)) * 8
    unit = LANES
    vmem = pltpu.VMEM
    dma = pltpu.SemaphoreType.DMA
    any_space = pl.BlockSpec(memory_space=pl.ANY)
    in_vmem = pl.BlockSpec(memory_space=pltpu.VMEM)
    return pl.pallas_call(
        functools.partial(kernel, n, layers, width, rank, span, piece, tokens),
        out_shape=(
            jax.ShapeDtypeStruct((CAP, 2 * rank, unit), jnp.bfloat16),
            jax.ShapeDtypeStruct((layers, 2, rank, rank), jnp.float32),
            jax.ShapeDtypeStruct((layers, 2, width), jnp.float32),
        ),
        in_specs=[any_space, any_space, pl.BlockSpec(memory_space=pltpu.SMEM)],
        out_specs=(any_space, in_vmem, in_vmem),
        scratch_shapes=[
            vmem((layers, width, span), jnp.bfloat16),
            vmem((layers, width, rank), jnp.bfloat16),
            vmem((layers, rank, span), jnp.bfloat16),
            vmem((2, CAP, rank, unit), jnp.bfloat16),
            vmem((8, LANES), jnp.int32),
            vmem((2, 8, LANES), jnp.int32),
            vmem((m * piece, LANES), jnp.float32),
            vmem((m, piece, LANES), jnp.float32),
            vmem((2, m * piece, LANES), jnp.float32),
            dma((layers,)), dma((layers,)), dma((layers, m)), dma((layers, m)),
            dma((2,)), dma((2,)), dma,
            dma((m,)), dma((m,)), dma((m,)), dma((m,)), dma, dma, dma((m,)), dma((m,)),
            dma((2, REACH)), dma((2, REACH)), dma((2,)),
        ],
        compiler_params=pltpu.CompilerParams(
            collective_id=0, has_side_effects=True, vmem_limit_bytes=40 * 1024 * 1024
        ),
        name="compress_handoff",
    )(key_values, bases, owner_slots)


def solution(mesh):
    in_specs = (P(None, "seq", "groups"), P(), P(None, ("groups", "seq")))
    out_specs = (
        P(("groups", "seq"), None, None),
        P("groups", None, None, None),
        P("groups", None, None),
    )
    return jax.shard_map(
        per_device, mesh=mesh, in_specs=in_specs, out_specs=out_specs, check_vma=False
    )
```

```python
import functools

import jax
import jax.numpy as jnp
from jax import lax
from jax.experimental import pallas as pl
from jax.experimental.pallas import tpu as pltpu
from jax.sharding import PartitionSpec as P

REACH = 8
OWNER_SLOT_LIMIT = 2
CAP = 16
LANES = 128
MESH = pl.DeviceIdType.MESH


def loop(lo, hi, body):
    def step(i, carry):
        body(i)
        return carry

    lax.fori_loop(lo, hi, step, 0)


def kernel(
    n, layers, width, rank, span, piece, tokens,
    kv_ref, bases_ref, slot_ref,
    recv_ref, grams_ref, energies_ref,
    x_buf, basis_buf, coeff_buf, out_buf, slot_mine, slot_buf, part_buf, pair_buf, sum_buf, full_buf,
    basis_sem, own_sem, x_send, x_recv, slot_send, slot_recv, slot_own,
    pair_send, pair_recv, rs_send, rs_recv, ag_send, ag_recv, mir_send, mir_recv, fwd_send, fwd_recv,
    sib_send, sib_recv, out_send, out_recv, out_own,
):
    m = n // 2
    chips = m // 2
    turn = n // 4
    chunk = 2 * width // n
    me = lax.axis_index("seq")
    side = me // m
    q = lax.rem(me, m)
    base = side * m
    chip = q // 2
    core = lax.rem(q, 2)
    sibling = me + 1 - 2 * core
    lrows = 2 * rank + width // LANES

    def remote(src, dst, send, recv, dev):
        return pltpu.make_async_remote_copy(
            src_ref=src, dst_ref=dst, send_sem=send, recv_sem=recv,
            device_id={"seq": dev}, device_id_type=MESH,
        )

    def held(i, dd):
        return lax.rem(2 * i + dd + n - turn, n)

    def holder(d):
        return lax.rem(d + turn, n) // 2

    def basis_copy(l):
        return pltpu.make_async_copy(bases_ref.at[l, side], basis_buf.at[l], basis_sem.at[l])

    def kv_at(l, i, dd):
        return kv_ref.at[l, :, pl.ds(pl.multiple_of(held(i, dd) * span, span), span)]

    def x_at(l, dd):
        return x_buf.at[dd, l, pl.ds(pl.multiple_of(q * chunk, chunk), chunk), :]

    def own_copy(l, dd):
        return pltpu.make_async_copy(kv_at(l, q, dd), x_at(l, dd), own_sem.at[dd, l])

    def x_copy(l, dd, r):
        to = lax.rem(q + r, m)
        return remote(
            kv_at(l, to, dd), x_at(l, dd), x_send.at[dd, l, r], x_recv.at[dd, l, r], base + to
        )

    barrier = pltpu.get_barrier_semaphore()

    def greet(r):
        pl.semaphore_signal(
            barrier, inc=1, device_id={"seq": lax.rem(me + r, n)}, device_id_type=MESH
        )

    loop(1, n, greet)
    for l in range(layers):
        basis_copy(l).start()
        for dd in range(2):
            own_copy(l, dd).start()
    slot_mine[...] = jnp.zeros(slot_mine.shape, jnp.int32)
    for l in range(layers):
        for b in range(2):
            slot_mine[2 * l + b : 2 * l + b + 1, :] = jnp.full((1, LANES), slot_ref[l, b], jnp.int32)
    pl.semaphore_wait(barrier, n - 1)

    for dd in range(2):
        for l in range(layers):
            loop(1, m, lambda r: x_copy(l, dd, r).start())

    lower = lax.rem(me + turn, 2)

    def slot_copy(hh):
        return remote(
            slot_mine, slot_buf.at[lower], slot_send.at[hh], slot_recv.at[lower],
            hh * m + holder(me),
        )

    def slot_local():
        return pltpu.make_async_copy(slot_mine, slot_buf.at[lower], slot_own)

    for hh in range(2):

        @pl.when(hh * m + holder(me) != me)
        def _():
            slot_copy(hh).start()

        @pl.when(hh * m + holder(me) == me)
        def _():
            slot_local().start()

    def out_dst(k):
        return recv_ref.at[
            pl.ds(OWNER_SLOT_LIMIT * k, OWNER_SLOT_LIMIT),
            pl.ds(pl.multiple_of(side * rank, rank), rank),
            :,
        ]

    def out_copy(dd, k):
        return remote(
            out_buf.at[dd, pl.ds(OWNER_SLOT_LIMIT * k, OWNER_SLOT_LIMIT)], out_dst(k),
            out_send.at[dd, k], out_recv.at[side, k], lax.rem(held(q, dd) + k, n),
        )

    def out_local(dd, k):
        return pltpu.make_async_copy(
            out_buf.at[dd, pl.ds(OWNER_SLOT_LIMIT * k, OWNER_SLOT_LIMIT)], out_dst(k), out_own.at[dd]
        )

    half_rows = chips * piece
    total_rows = m * piece
    if total_rows > layers * lrows:
        part_buf[layers * lrows :, :] = jnp.zeros(
            (total_rows - layers * lrows, LANES), jnp.float32
        )

    def half_of(b):
        return pl.ds(pl.multiple_of(b * half_rows, piece), half_rows)

    def rows_of(c):
        return pl.ds(pl.multiple_of(core * half_rows + c * piece, piece), piece)

    def pair_copy():
        return remote(part_buf.at[half_of(1 - core), :], pair_buf, pair_send, pair_recv, sibling)

    def emit(dd, ks):
        src_dev = held(q, dd)
        for k in ks:
            for w in range(OWNER_SLOT_LIMIT):
                v = OWNER_SLOT_LIMIT * k + w
                acc = None
                for l in range(layers):
                    for b in range(2):
                        pick = slot_buf[dd, 2 * l + b : 2 * l + b + 1, :] == v
                        pick = pick.astype(jnp.float32).astype(jnp.bfloat16)
                        term = coeff_buf[l, :, b * LANES : (b + 1) * LANES] * pick
                        acc = term if acc is None else acc + term
                out_buf[dd, v] = acc
            to = lax.rem(src_dev + k, n)

            @pl.when(to != me)
            def _():
                out_copy(dd, k).start()

            @pl.when(to == me)
            def _():
                out_local(dd, k).start()

    def rs_copy(r):
        to = lax.rem(chip + r, chips)
        return remote(
            part_buf.at[rows_of(to), :], sum_buf.at[r], rs_send.at[r], rs_recv.at[r],
            base + 2 * to + core,
        )

    def ag_copy(r):
        at = full_buf.at[side, rows_of(chip), :]
        return remote(
            at, at, ag_send.at[r], ag_recv.at[r], base + 2 * lax.rem(chip + r, chips) + core
        )

    def mirror_copy():
        at = full_buf.at[side, rows_of(chip), :]
        return remote(at, at, mir_send, mir_recv, (1 - side) * m + q)

    def fwd_copy(r):
        at = full_buf.at[1 - side, rows_of(chip), :]
        return remote(
            at, at, fwd_send.at[r], fwd_recv.at[r], base + 2 * lax.rem(chip + r, chips) + core
        )

    def sib_copy(s):
        at = full_buf.at[s, half_of(core), :]
        return remote(at, at, sib_send.at[s], sib_recv.at[s], sibling)

    for dd in range(2):
        for l in range(layers):
            if dd == 0:
                basis_copy(l).wait()
            own_copy(l, dd).wait()
            loop(1, m, lambda r: x_copy(l, dd, r).wait_recv())
            coeff = lax.dot_general(
                basis_buf[l], x_buf[dd, l], (((0,), (0,)), ((), ())),
                preferred_element_type=jnp.float32,
            ).astype(jnp.bfloat16)
            coeff_buf[l] = coeff
            gram = lax.dot_general(
                coeff, coeff, (((1,), (1,)), ((), ())), preferred_element_type=jnp.float32
            )

            def put(at, value):
                if dd == 0:
                    part_buf[at : at + value.shape[0], :] = value
                else:
                    part_buf[at : at + value.shape[0], :] += value

            top = l * lrows
            for j in range(rank // LANES):
                put(top + j * rank, gram[:, j * LANES : (j + 1) * LANES])
            top += 2 * rank
            rows = 256
            for c in range(width // rows):
                recon = jnp.dot(
                    basis_buf[l, c * rows : (c + 1) * rows, :], coeff,
                    preferred_element_type=jnp.float32,
                )
                resid = x_buf[dd, l, c * rows : (c + 1) * rows, :].astype(jnp.float32) - recon
                square = resid * resid
                folded = square[:, :LANES]
                for j in range(1, span // LANES):
                    folded = folded + square[:, j * LANES : (j + 1) * LANES]
                line = jnp.sum(folded.T, axis=0, keepdims=True)
                for j in range(rows // LANES):
                    put(top + c * (rows // LANES) + j, line[:, j * LANES : (j + 1) * LANES])

        if dd == 1:
            pair_copy().start()

        src_dev = held(q, dd)

        @pl.when(src_dev != me)
        def _():
            remote(slot_mine, slot_buf.at[dd], slot_send.at[0], slot_recv.at[dd], me).wait_recv()

        @pl.when(src_dev == me)
        def _():
            pltpu.make_async_copy(slot_mine, slot_buf.at[dd], slot_own).wait()

        if dd == 0:
            emit(0, range(REACH - 1, -1, -1))

    ks = list(range(REACH - 1, -1, -1))
    emit(1, ks[:2])
    pair_copy().wait()
    part_buf[half_of(core), :] += pair_buf[...]
    loop(1, chips, lambda r: rs_copy(r).start())
    emit(1, ks[2:4])
    loop(1, chips, lambda r: rs_copy(r).wait())
    total = part_buf[rows_of(chip), :]
    for r in range(1, chips):
        total = total + sum_buf[r]
    full_buf[side, rows_of(chip), :] = total
    mirror_copy().start()
    loop(1, chips, lambda r: ag_copy(r).start())
    emit(1, ks[4:6])
    loop(1, chips, lambda r: ag_copy(r).wait_recv())
    sib_copy(side).start()
    mirror_copy().wait_recv()
    loop(1, chips, lambda r: fwd_copy(r).start())
    emit(1, ks[6:])
    loop(1, chips, lambda r: fwd_copy(r).wait_recv())
    sib_copy(1 - side).start()
    sib_copy(0).wait()
    sib_copy(1).wait()

    scale = 1.0 / tokens
    for s in range(2):
        for l in range(layers):
            top = l * lrows
            for j in range(rank // LANES):
                grams_ref[l, s, :, j * LANES : (j + 1) * LANES] = (
                    full_buf[s, top + j * rank : top + (j + 1) * rank, :] * scale
                )
            top += 2 * rank
            for j in range(width // LANES):
                energies_ref[l, s : s + 1, j * LANES : (j + 1) * LANES] = (
                    full_buf[s, top + j : top + j + 1, :] * scale
                )

    mirror_copy().wait_send()
    loop(1, chips, lambda r: ag_copy(r).wait_send())
    loop(1, chips, lambda r: fwd_copy(r).wait_send())
    for hh in range(2):

        @pl.when(hh * m + holder(me) != me)
        def _():
            slot_copy(hh).wait_send()

    for dd in range(2):
        for l in range(layers):
            loop(1, m, lambda r: x_copy(l, dd, r).wait_send())
        for k in range(REACH):
            to = lax.rem(held(q, dd) + k, n)

            @pl.when(to != me)
            def _():
                out_copy(dd, k).wait_send()

            @pl.when(to == me)
            def _():
                out_local(dd, k).wait()

    for hh in range(2):
        for k in range(REACH):
            sender = hh * m + holder(lax.rem(me - k + n, n))

            @pl.when(sender != me)
            def _():
                at = recv_ref.at[
                    pl.ds(OWNER_SLOT_LIMIT * k, OWNER_SLOT_LIMIT), pl.ds(hh * rank, rank), :
                ]
                remote(at, at, out_send.at[0, 0], out_recv.at[hh, k], me).wait_recv()


def per_device(key_values, bases, owner_slots):
    n = lax.axis_size("seq")
    layers, chunk, tokens = key_values.shape
    width, rank = bases.shape[2], bases.shape[3]
    m = n // 2
    chips = m // 2
    span = tokens // n
    lrows = 2 * rank + width // LANES
    piece = -(-layers * lrows // (8 * m)) * 8
    unit = LANES
    vmem = pltpu.VMEM
    dma = pltpu.SemaphoreType.DMA
    any_space = pl.BlockSpec(memory_space=pl.ANY)
    in_vmem = pl.BlockSpec(memory_space=pltpu.VMEM)
    return pl.pallas_call(
        functools.partial(kernel, n, layers, width, rank, span, piece, tokens),
        out_shape=(
            jax.ShapeDtypeStruct((CAP, 2 * rank, unit), jnp.bfloat16),
            jax.ShapeDtypeStruct((layers, 2, rank, rank), jnp.float32),
            jax.ShapeDtypeStruct((layers, 2, width), jnp.float32),
        ),
        in_specs=[any_space, any_space, pl.BlockSpec(memory_space=pltpu.SMEM)],
        out_specs=(any_space, in_vmem, in_vmem),
        scratch_shapes=[
            vmem((2, layers, width, span), jnp.bfloat16),
            vmem((layers, width, rank), jnp.bfloat16),
            vmem((layers, rank, span), jnp.bfloat16),
            vmem((2, CAP, rank, unit), jnp.bfloat16),
            vmem((8, LANES), jnp.int32),
            vmem((2, 8, LANES), jnp.int32),
            vmem((m * piece, LANES), jnp.float32),
            vmem((chips * piece, LANES), jnp.float32),
            vmem((chips, piece, LANES), jnp.float32),
            vmem((2, m * piece, LANES), jnp.float32),
            dma((layers,)), dma((2, layers)), dma((2, layers, m)), dma((2, layers, m)),
            dma((2,)), dma((2,)), dma,
            dma, dma, dma((chips,)), dma((chips,)), dma((chips,)), dma((chips,)), dma, dma,
            dma((chips,)), dma((chips,)),
            dma((2,)), dma((2,)), dma((2, REACH)), dma((2, REACH)), dma((2,)),
        ],
        compiler_params=pltpu.CompilerParams(
            collective_id=0, has_side_effects=True, vmem_limit_bytes=58 * 1024 * 1024
        ),
        name="compress_handoff",
    )(key_values, bases, owner_slots)


def solution(mesh):
    in_specs = (P(None, "seq", "groups"), P(), P(None, ("groups", "seq")))
    out_specs = (
        P(("groups", "seq"), None, None),
        P("groups", None, None, None),
        P("groups", None, None),
    )
    return jax.shard_map(
        per_device, mesh=mesh, in_specs=in_specs, out_specs=out_specs, check_vma=False
    )
```

```python
import functools

import jax
import jax.numpy as jnp
from jax import lax
from jax.experimental import pallas as pl
from jax.experimental.pallas import tpu as pltpu
from jax.sharding import PartitionSpec as P

REACH = 8
OWNER_SLOT_LIMIT = 2
CAP = 16
LANES = 128
MESH = pl.DeviceIdType.MESH


def loop(lo, hi, body):
    def step(i, carry):
        body(i)
        return carry

    lax.fori_loop(lo, hi, step, 0)


def kernel(
    n, layers, width, rank, span, piece, tokens,
    kv_ref, bases_ref, slot_ref,
    recv_ref, grams_ref, energies_ref,
    x_buf, basis_buf, coeff_buf, raw_buf, out_buf, slot_mine, slot_buf, raw_slot, part_buf, pair_buf, sum_buf, full_buf,
    basis_sem, own_sem, x_send, x_recv, slot_send, slot_recv, slot_own,
    pair_send, pair_recv, rs_send, rs_recv, ag_send, ag_recv, mir_send, mir_recv, fwd_send, fwd_recv,
    sib_send, sib_recv, raw_send, raw_recv, raw_slot_send, raw_slot_recv, out_send, out_recv, out_own,
):
    m = n // 2
    chips = m // 2
    turn = n // 4
    chunk = 2 * width // n
    me = lax.axis_index("seq")
    side = me // m
    q = lax.rem(me, m)
    base = side * m
    chip = q // 2
    core = lax.rem(q, 2)
    sibling = me + 1 - 2 * core
    lrows = 2 * rank + width // LANES
    step = (1 - 2 * side) * (m // 2)
    partner = me + step
    partner_q = q - step
    inner = q // (m // 2) == 1 - side

    def remote(src, dst, send, recv, dev):
        return pltpu.make_async_remote_copy(
            src_ref=src, dst_ref=dst, send_sem=send, recv_sem=recv,
            device_id={"seq": dev}, device_id_type=MESH,
        )

    def held(i, dd):
        return lax.rem(2 * i + dd + n - turn, n)

    def holder(d):
        return lax.rem(d + turn, n) // 2

    def basis_copy(l):
        return pltpu.make_async_copy(bases_ref.at[l, side], basis_buf.at[l], basis_sem.at[l])

    def kv_at(l, i, dd):
        return kv_ref.at[l, :, pl.ds(pl.multiple_of(held(i, dd) * span, span), span)]

    def x_at(l, dd):
        return x_buf.at[dd, l, pl.ds(pl.multiple_of(q * chunk, chunk), chunk), :]

    def own_copy(l, dd):
        return pltpu.make_async_copy(kv_at(l, q, dd), x_at(l, dd), own_sem.at[dd, l])

    def x_copy(l, dd, r):
        to = lax.rem(q + r, m)
        return remote(
            kv_at(l, to, dd), x_at(l, dd), x_send.at[dd, l, r], x_recv.at[dd, l, r], base + to
        )

    barrier = pltpu.get_barrier_semaphore()

    def greet(r):
        pl.semaphore_signal(
            barrier, inc=1, device_id={"seq": lax.rem(me + r, n)}, device_id_type=MESH
        )

    loop(1, n, greet)
    for l in range(layers):
        basis_copy(l).start()
        for dd in range(2):
            own_copy(l, dd).start()
    slot_mine[...] = jnp.zeros(slot_mine.shape, jnp.int32)
    for l in range(layers):
        for b in range(2):
            slot_mine[2 * l + b : 2 * l + b + 1, :] = jnp.full((1, LANES), slot_ref[l, b], jnp.int32)
    pl.semaphore_wait(barrier, n - 1)

    for dd in range(2):
        for l in range(layers):
            loop(1, m, lambda r: x_copy(l, dd, r).start())

    lower = lax.rem(me + turn, 2)

    def slot_copy(hh):
        return remote(
            slot_mine, slot_buf.at[lower], slot_send.at[hh], slot_recv.at[lower],
            hh * m + holder(me),
        )

    def slot_local():
        return pltpu.make_async_copy(slot_mine, slot_buf.at[lower], slot_own)

    for hh in range(2):

        @pl.when(hh * m + holder(me) != me)
        def _():
            slot_copy(hh).start()

        @pl.when(hh * m + holder(me) == me)
        def _():
            slot_local().start()

    def raw_copy(dd, l):
        return remote(
            coeff_buf.at[dd, l], raw_buf.at[dd, l], raw_send.at[dd, l], raw_recv.at[dd, l], partner
        )

    def raw_slot_copy(dd):
        return remote(
            slot_buf.at[dd], raw_slot.at[dd], raw_slot_send.at[dd], raw_slot_recv.at[dd], partner
        )

    def owner(relay, dd, k):
        return lax.rem(held(partner_q if relay else q, dd) + k, n)

    def is_sent(relay, dd, k):
        near = owner(relay, dd, k) // m == side
        if relay:
            return jnp.logical_and(inner, near)
        return jnp.logical_or(jnp.logical_not(inner), near)

    def out_refs(relay, dd, k):
        part = 1 - side if relay else side
        slots = pl.ds(OWNER_SLOT_LIMIT * k, OWNER_SLOT_LIMIT)
        dst = recv_ref.at[slots, pl.ds(pl.multiple_of(part * rank, rank), rank), :]
        return part, out_buf.at[int(relay), dd, slots], dst

    def out_copy(relay, dd, k):
        part, src, dst = out_refs(relay, dd, k)
        return remote(
            src, dst, out_send.at[int(relay), dd, k], out_recv.at[part, k], owner(relay, dd, k)
        )

    def out_local(relay, dd, k):
        part, src, dst = out_refs(relay, dd, k)
        return pltpu.make_async_copy(src, dst, out_own.at[int(relay), dd])

    half_rows = chips * piece
    total_rows = m * piece
    if total_rows > layers * lrows:
        part_buf[layers * lrows :, :] = jnp.zeros(
            (total_rows - layers * lrows, LANES), jnp.float32
        )

    def half_of(b):
        return pl.ds(pl.multiple_of(b * half_rows, piece), half_rows)

    def rows_of(c):
        return pl.ds(pl.multiple_of(core * half_rows + c * piece, piece), piece)

    def pair_copy():
        return remote(part_buf.at[half_of(1 - core), :], pair_buf, pair_send, pair_recv, sibling)

    def emit(relay, dd, ks):
        units = raw_buf if relay else coeff_buf
        numbers = raw_slot if relay else slot_buf
        for k in ks:

            @pl.when(is_sent(relay, dd, k))
            def _():
                for w in range(OWNER_SLOT_LIMIT):
                    v = OWNER_SLOT_LIMIT * k + w
                    acc = None
                    for l in range(layers):
                        for b in range(2):
                            pick = numbers[dd, 2 * l + b : 2 * l + b + 1, :] == v
                            pick = pick.astype(jnp.float32).astype(jnp.bfloat16)
                            term = units[dd, l, :, b * LANES : (b + 1) * LANES] * pick
                            acc = term if acc is None else acc + term
                    out_buf[int(relay), dd, v] = acc

                @pl.when(owner(relay, dd, k) != me)
                def _():
                    out_copy(relay, dd, k).start()

                @pl.when(owner(relay, dd, k) == me)
                def _():
                    out_local(relay, dd, k).start()

    def take_raw(dd):
        @pl.when(inner)
        def _():
            for l in range(layers):
                raw_copy(dd, l).wait_recv()
            raw_slot_copy(dd).wait_recv()

    def rs_copy(r):
        to = lax.rem(chip + r, chips)
        return remote(
            part_buf.at[rows_of(to), :], sum_buf.at[r], rs_send.at[r], rs_recv.at[r],
            base + 2 * to + core,
        )

    def ag_copy(r):
        at = full_buf.at[side, rows_of(chip), :]
        return remote(
            at, at, ag_send.at[r], ag_recv.at[r], base + 2 * lax.rem(chip + r, chips) + core
        )

    def mirror_copy():
        at = full_buf.at[side, rows_of(chip), :]
        return remote(at, at, mir_send, mir_recv, (1 - side) * m + q)

    def fwd_copy(r):
        at = full_buf.at[1 - side, rows_of(chip), :]
        return remote(
            at, at, fwd_send.at[r], fwd_recv.at[r], base + 2 * lax.rem(chip + r, chips) + core
        )

    def sib_copy(s):
        at = full_buf.at[s, half_of(core), :]
        return remote(at, at, sib_send.at[s], sib_recv.at[s], sibling)

    ks = list(range(REACH - 1, -1, -1))
    for dd in range(2):
        for l in range(layers):
            if dd == 1 and l == layers - 1:
                take_raw(0)
                emit(True, 0, ks)
            if dd == 0:
                basis_copy(l).wait()
            own_copy(l, dd).wait()
            loop(1, m, lambda r: x_copy(l, dd, r).wait_recv())
            coeff = lax.dot_general(
                basis_buf[l], x_buf[dd, l], (((0,), (0,)), ((), ())),
                preferred_element_type=jnp.float32,
            ).astype(jnp.bfloat16)
            coeff_buf[dd, l] = coeff

            @pl.when(inner)
            def _():
                raw_copy(dd, l).start()

            gram = lax.dot_general(
                coeff, coeff, (((1,), (1,)), ((), ())), preferred_element_type=jnp.float32
            )

            def put(at, value):
                if dd == 0:
                    part_buf[at : at + value.shape[0], :] = value
                else:
                    part_buf[at : at + value.shape[0], :] += value

            top = l * lrows
            for j in range(rank // LANES):
                put(top + j * rank, gram[:, j * LANES : (j + 1) * LANES])
            top += 2 * rank
            rows = 256
            for c in range(width // rows):
                recon = jnp.dot(
                    basis_buf[l, c * rows : (c + 1) * rows, :], coeff,
                    preferred_element_type=jnp.float32,
                )
                resid = x_buf[dd, l, c * rows : (c + 1) * rows, :].astype(jnp.float32) - recon
                square = resid * resid
                folded = square[:, :LANES]
                for j in range(1, span // LANES):
                    folded = folded + square[:, j * LANES : (j + 1) * LANES]
                line = jnp.sum(folded.T, axis=0, keepdims=True)
                for j in range(rows // LANES):
                    put(top + c * (rows // LANES) + j, line[:, j * LANES : (j + 1) * LANES])

        if dd == 1:
            pair_copy().start()

        src_dev = held(q, dd)

        @pl.when(src_dev != me)
        def _():
            remote(slot_mine, slot_buf.at[dd], slot_send.at[0], slot_recv.at[dd], me).wait_recv()

        @pl.when(src_dev == me)
        def _():
            pltpu.make_async_copy(slot_mine, slot_buf.at[dd], slot_own).wait()

        @pl.when(inner)
        def _():
            raw_slot_copy(dd).start()

        if dd == 0:
            emit(False, 0, ks)

    pair_copy().wait()
    part_buf[half_of(core), :] += pair_buf[...]
    loop(1, chips, lambda r: rs_copy(r).start())
    loop(1, chips, lambda r: rs_copy(r).wait())
    total = part_buf[rows_of(chip), :]
    for r in range(1, chips):
        total = total + sum_buf[r]
    full_buf[side, rows_of(chip), :] = total
    mirror_copy().start()
    loop(1, chips, lambda r: ag_copy(r).start())
    emit(False, 1, ks[:4])
    emit(False, 1, ks[4:])
    loop(1, chips, lambda r: ag_copy(r).wait_recv())
    sib_copy(side).start()
    mirror_copy().wait_recv()
    loop(1, chips, lambda r: fwd_copy(r).start())
    take_raw(1)
    emit(True, 1, ks[:4])
    emit(True, 1, ks[4:])
    loop(1, chips, lambda r: fwd_copy(r).wait_recv())
    sib_copy(1 - side).start()
    sib_copy(0).wait()
    sib_copy(1).wait()

    scale = 1.0 / tokens
    for s in range(2):
        for l in range(layers):
            top = l * lrows
            for j in range(rank // LANES):
                grams_ref[l, s, :, j * LANES : (j + 1) * LANES] = (
                    full_buf[s, top + j * rank : top + (j + 1) * rank, :] * scale
                )
            top += 2 * rank
            for j in range(width // LANES):
                energies_ref[l, s : s + 1, j * LANES : (j + 1) * LANES] = (
                    full_buf[s, top + j : top + j + 1, :] * scale
                )

    mirror_copy().wait_send()
    loop(1, chips, lambda r: ag_copy(r).wait_send())
    loop(1, chips, lambda r: fwd_copy(r).wait_send())
    for hh in range(2):

        @pl.when(hh * m + holder(me) != me)
        def _():
            slot_copy(hh).wait_send()

    for dd in range(2):
        for l in range(layers):
            loop(1, m, lambda r: x_copy(l, dd, r).wait_send())
        @pl.when(inner)
        def _():
            for l in range(layers):
                raw_copy(dd, l).wait_send()
            raw_slot_copy(dd).wait_send()

        for relay in (False, True):
            for k in range(REACH):
                sent = is_sent(relay, dd, k)
                away = owner(relay, dd, k) != me

                @pl.when(jnp.logical_and(sent, away))
                def _():
                    out_copy(relay, dd, k).wait_send()

                @pl.when(jnp.logical_and(sent, jnp.logical_not(away)))
                def _():
                    out_local(relay, dd, k).wait()

    for hh in range(2):
        for k in range(REACH):
            held_by = holder(lax.rem(me - k + n, n))
            relayed = jnp.logical_and(side != hh, held_by // (m // 2) == 1 - hh)
            sender = hh * m + held_by + jnp.where(relayed, (1 - 2 * hh) * (m // 2), 0)

            @pl.when(sender != me)
            def _():
                at = recv_ref.at[
                    pl.ds(OWNER_SLOT_LIMIT * k, OWNER_SLOT_LIMIT), pl.ds(hh * rank, rank), :
                ]
                remote(at, at, out_send.at[0, 0, 0], out_recv.at[hh, k], me).wait_recv()


def per_device(key_values, bases, owner_slots):
    n = lax.axis_size("seq")
    layers, chunk, tokens = key_values.shape
    width, rank = bases.shape[2], bases.shape[3]
    m = n // 2
    chips = m // 2
    span = tokens // n
    lrows = 2 * rank + width // LANES
    piece = -(-layers * lrows // (8 * m)) * 8
    unit = LANES
    vmem = pltpu.VMEM
    dma = pltpu.SemaphoreType.DMA
    any_space = pl.BlockSpec(memory_space=pl.ANY)
    in_vmem = pl.BlockSpec(memory_space=pltpu.VMEM)
    return pl.pallas_call(
        functools.partial(kernel, n, layers, width, rank, span, piece, tokens),
        out_shape=(
            jax.ShapeDtypeStruct((CAP, 2 * rank, unit), jnp.bfloat16),
            jax.ShapeDtypeStruct((layers, 2, rank, rank), jnp.float32),
            jax.ShapeDtypeStruct((layers, 2, width), jnp.float32),
        ),
        in_specs=[any_space, any_space, pl.BlockSpec(memory_space=pltpu.SMEM)],
        out_specs=(any_space, in_vmem, in_vmem),
        scratch_shapes=[
            vmem((2, layers, width, span), jnp.bfloat16),
            vmem((layers, width, rank), jnp.bfloat16),
            vmem((2, layers, rank, span), jnp.bfloat16),
            vmem((2, layers, rank, span), jnp.bfloat16),
            vmem((2, 2, CAP, rank, unit), jnp.bfloat16),
            vmem((8, LANES), jnp.int32),
            vmem((2, 8, LANES), jnp.int32),
            vmem((2, 8, LANES), jnp.int32),
            vmem((m * piece, LANES), jnp.float32),
            vmem((chips * piece, LANES), jnp.float32),
            vmem((chips, piece, LANES), jnp.float32),
            vmem((2, m * piece, LANES), jnp.float32),
            dma((layers,)), dma((2, layers)), dma((2, layers, m)), dma((2, layers, m)),
            dma((2,)), dma((2,)), dma,
            dma, dma, dma((chips,)), dma((chips,)), dma((chips,)), dma((chips,)), dma, dma,
            dma((chips,)), dma((chips,)),
            dma((2,)), dma((2,)), dma((2, layers)), dma((2, layers)), dma((2,)), dma((2,)),
            dma((2, 2, REACH)), dma((2, REACH)), dma((2, 2)),
        ],
        compiler_params=pltpu.CompilerParams(
            collective_id=0, has_side_effects=True, vmem_limit_bytes=58 * 1024 * 1024
        ),
        name="compress_handoff",
    )(key_values, bases, owner_slots)


def solution(mesh):
    in_specs = (P(None, "seq", "groups"), P(), P(None, ("groups", "seq")))
    out_specs = (
        P(("groups", "seq"), None, None),
        P("groups", None, None, None),
        P("groups", None, None),
    )
    return jax.shard_map(
        per_device, mesh=mesh, in_specs=in_specs, out_specs=out_specs, check_vma=False
    )
```
